32 devices in a mesh: tok: 16 (over z, y, x), hid: 2 (over core).
Axes of the slice: x: 2, y: 2, z: 4, core: 2. Of those that a mesh axis runs over, the one named last changes fastest.
Arguments:
- acts: bfloat16 [4096, 28672], P('tok', 'hid'), may hold values from -6 to 6
- out_grads: bfloat16 [4096, 8192], P('tok', 'hid'), may hold values from -0.119628906 to 0.119628906
- proj_in: bfloat16 [28672, 64], P('hid'), may hold values from -0.03125 to 0.03125
- proj_out: bfloat16 [8192, 64], P('hid'), may hold values from -0.0625 to 0.0625
- example_ids: int32 [4096], P('tok'), may hold values from 0 to 3, never falling along the last dimension, each value on 1 to 2048 neighbouring positions
- queries: float32 [1024, 4096], P(None, 'tok'), may hold values from -0.09375 to 0.09375
- precond: float32 [4096, 4096], P('tok', 'hid'), may hold values from -0.09375 to 0.09375
Outputs:
- scores: float32 [1024, 4], P('tok')
- features: float32 [4, 4096], P(None, 'hid')
The draws below stay inside these ranges and needn't reach their ends.
Inputs may be any that keep to these rules, and one draw needn't show every extreme that they name: `example_ids`: ids never fall along the tokens; each example holds 1 to 2048 tokens, and one holds exactly 2048.
All inputs are finite; a program needn't handle non-finite values.
Results may differ from the reference program's by a relative error of at most 0.0003.
Values sent between devices are 32-bit elements; how exact they have to be, the bound alone decides.
A program may use at most 64 MiB of HBM per device.

```python
import math
import jax
import jax.numpy as jnp
import numpy as np
from jax import lax

D = 8192
FF = 28672
R = 64
QUERIES = 1024
EX_LEN = 2048
TOKENS = 4096
EXAMPLES = 4
F = 4096


def level_of(own_key, dims, shards, low, top_value):
    level = 1.0
    for position, shards_of in shards:
        heights = jax.random.uniform(jax.random.fold_in(jax.random.fold_in(own_key, 6), position), (shards_of,), jnp.float32, low / len(shards), top_value / len(shards))
        level = level * jnp.repeat(jnp.exp(heights), dims[position] // shards_of).reshape((-1,) + (1,) * (len(dims) - 1 - position))
    return level


def length_profile(number_of, total, most, slope):
    weights = [(1 << 20) // math.isqrt(rank ** slope) + 1 for rank in range(2, number_of + 1)]
    surplus, counts = total - most - (number_of - 1), [1] * (number_of - 1)
    while surplus > 0:
        candidates = [i for i in range(number_of - 1) if counts[i] < most]
        pool, remaining = sum([weights[i] for i in candidates]), surplus
        for i in candidates:
            addition = min(most - counts[i], max(1, remaining * weights[i] // pool), surplus)
            counts[i] = counts[i] + addition
            surplus = surplus - addition
    return np.array([most] + counts)


def ragged(key, number_of, total, limit, skew):
    if number_of == 2:
        one = jax.random.randint(key, (), max(1, total - limit), min(limit, total - 1) + 1)
        return jnp.stack([one, total - one])
    sizes = jnp.asarray(length_profile(number_of, total, limit, skew), jnp.int32)
    couples = (number_of - 1) // 2
    donor, sink = sizes[1:1 + 2 * couples:2], sizes[2:2 + 2 * couples:2]
    room = jnp.minimum(donor - 1, limit - sink)
    shifted = jax.random.randint(jax.random.fold_in(key, 1), (couples,), 0, 1 << 20) % (room + 1)
    sizes = sizes.at[1:1 + 2 * couples:2].set(donor - shifted).at[2:2 + 2 * couples:2].set(sink + shifted)
    return sizes[jax.random.permutation(jax.random.fold_in(key, 2), number_of)]


def centred(stream_key, shape, scale, most, pieces=(), kind=jnp.bfloat16):
    result = jax.random.normal(stream_key, shape, jnp.float32) * scale
    if len(pieces) > 0:
        result = level_of(stream_key, shape, pieces, -0.22, 0.18) * result
    return jnp.clip(result, min=-most, max=most).astype(kind)


def setup_inputs(seed: int = 0) -> dict:
    splits = jax.random.split(jax.random.key(seed), 8)
    acts = centred(splits[0], (TOKENS, FF), 1.0, 6.0, ((0, 16), (1, 2)))
    out_grads = centred(splits[1], (TOKENS, D), 0.02, 0.119628906, ((0, 16), (1, 2)))
    proj_in = centred(splits[2], (FF, R), FF ** -0.5, 0.03125, ((0, 2),))
    proj_out = centred(splits[3], (D, R), D ** -0.5, 0.0625, ((0, 2),))
    example_ids = jnp.searchsorted(jnp.cumsum(ragged(splits[4], EXAMPLES, TOKENS, EX_LEN, 0)), jnp.arange(TOKENS), side="right").astype(jnp.int32)
    queries = centred(splits[5], (QUERIES, F), F ** -0.5, 0.09375, ((1, 16),), jnp.float32)
    precond = centred(splits[6], (F, F), F ** -0.5, 0.09375, ((0, 16), (1, 2)), jnp.float32)
    return dict(acts=acts, out_grads=out_grads, proj_in=proj_in, proj_out=proj_out, example_ids=example_ids, queries=queries, precond=precond)


def reference(acts, out_grads, proj_in, proj_out, example_ids, queries, precond):
    inner = jnp.dot(acts, proj_in, preferred_element_type=jnp.float32)
    outer = jnp.dot(out_grads, proj_out, preferred_element_type=jnp.float32)
    onehot = (example_ids[:, None] == jnp.arange(EXAMPLES, dtype=jnp.int32)[None, :]).astype(jnp.float32)
    weighted = (onehot[:, :, None] * inner[:, None, :]).reshape(inner.shape[0], EXAMPLES * R)
    feats = lax.dot_general(weighted, outer, (((0,), (0,)), ((), ())), precision=lax.Precision.HIGHEST, preferred_element_type=jnp.float32)
    feats = feats.reshape(EXAMPLES, R * R)
    image = jnp.dot(precond, feats.T, precision=lax.Precision.HIGHEST, preferred_element_type=jnp.float32)
    scores = jnp.dot(queries, image, precision=lax.Precision.HIGHEST, preferred_element_type=jnp.float32)
    return scores, feats
```

```python
import functools

import jax
import jax.numpy as jnp
from jax import lax
from jax.experimental import pallas as pl
from jax.experimental.pallas import tpu as pltpu
from jax.sharding import PartitionSpec as P

EX_LEN = 2048
TILE = 256
MESH = pl.DeviceIdType.MESH
BF, F32 = jnp.bfloat16, jnp.float32


def split(x):
    hi = x.astype(BF)
    return hi, (x - hi.astype(F32)).astype(BF)


def fill(pair, src, at):
    for ref in pair:
        if ref.shape != src.shape:
            ref[...] = jnp.zeros(ref.shape, BF)
    for ref, half in zip(pair, split(src[...])):
        ref[at] = half


def kernel(
    T, H, A, E, ci, co,
    acts, grads, pin, pout, ids, queries, precond,
    scores_out, feats_out,
    acts_v, grads_v, pin_v, pout_v, ids_v, q_v, p_v,
    q_hi, q_lo, p_hi, p_lo,
    inner_v, outer_v, inner_r, outer_r, r_v, w_v, y_v, rs_r, z_v, own_v, full_v,
    f2_v, im2_v, sc_v, s_v,
    ld_sem, in_sem, hs_sem, hr_sem, as_sem, ar_sem, zs_sem, zr_sem, gs_sem, gr_sem,
    ss_sem, sr_sem,
):
    B = T // A
    t, h = lax.axis_index("tok"), lax.axis_index("hid")
    a, b = lax.rem(t, A), lax.div(t, A)
    width, tokens = inner_v.shape
    slab = width // H
    half = slab // 2
    part = half // A

    loads = {}

    def load(name, src, dst):
        c = pltpu.make_async_copy(src, dst, ld_sem.at[len(loads)])
        c.start()
        loads[name] = c

    load("pout", pout, pout_v)
    go = grads.shape[1] // co
    for c in range(co):
        k = pl.ds(c * go, go)
        load(("g", c), grads.at[:, k], grads_v.at[:, k])
    gi = acts.shape[1] // ci
    for c in range(ci):
        k = pl.ds(c * gi, gi)
        load(("pi", c), pin.at[:, k], pin_v.at[:, k])
        load(("a", c), acts.at[:, k], acts_v.at[:, k])
    load("ids", ids, ids_v)
    load("p", precond, p_v)
    load("q", queries, q_v)

    def peer(d):
        return lax.rem(t + d // H, T), lax.rem(h + d % H, H)

    barrier = pltpu.get_barrier_semaphore()
    everyone = T * H - 1

    def greet(d, _):
        pt = lax.rem(t + lax.div(d, H), T)
        ph = lax.rem(h + lax.rem(d, H), H)
        pl.semaphore_signal(barrier, inc=1, device_id=(pt, ph), device_id_type=MESH)
        return 0

    lax.fori_loop(1, T * H, greet, 0, unroll=T * H <= 32)

    hid_out, hid_in = [], []
    for d in range(1, H):
        hid_out.append(pltpu.make_async_remote_copy(
            outer_v, outer_r.at[d - 1], hs_sem.at[0, d - 1], hr_sem.at[0, d - 1],
            device_id=(t, lax.rem(h + d, H)), device_id_type=MESH))

    def project(*accs):
        step = 0

        def tiles(x, y, start, size, pair):
            nonlocal step
            for j in range(0, size, TILE):
                k = pl.ds(start + j, TILE)
                unit, slot = step % 2, step // 2 % 2
                pltpu.matmul_push_rhs(y[:, k], slot, unit, transpose=True)
                pltpu.matmul_acc_lhs(pair[unit], x[:, k], slot)
                step += 1

        loads["pout"].wait()
        for c in range(co):
            loads[("g", c)].wait()
            tiles(pout_v, grads_v, c * go, go, accs[:2])
        outer_v[...] = pltpu.matmul_pop(accs[0]) + pltpu.matmul_pop(accs[1])
        for c in range(ci):
            if c == ci - 1:
                pl.semaphore_wait(barrier, everyone)
                for cp in hid_out:
                    cp.start()
            loads[("pi", c)].wait()
            loads[("a", c)].wait()
            tiles(pin_v, acts_v, c * gi, gi, accs[2:])
        inner_v[...] = pltpu.matmul_pop(accs[2]) + pltpu.matmul_pop(accs[3])

    pl.run_scoped(project, *[pltpu.ACC(u)((width, tokens), F32) for u in (0, 1, 0, 1)])
    for d in range(1, H):
        ph = lax.rem(h + d, H)
        cp = pltpu.make_async_remote_copy(
            inner_v.at[pl.ds(pl.multiple_of(ph * slab, slab), slab), :], inner_r.at[d - 1],
            hs_sem.at[1, d - 1], hr_sem.at[1, d - 1],
            device_id=(t, ph), device_id_type=MESH)
        cp.start()
        hid_in.append(cp)
    loads["ids"].wait()

    for cp in hid_out:
        cp.wait_recv()
    outer = outer_v[...]
    for d in range(1, H):
        outer = outer + outer_r[d - 1]
    o_hi, o_lo = split(jnp.concatenate([outer, outer], axis=0))
    for cp in hid_in:
        cp.wait_recv()
    inner = inner_v[pl.ds(pl.multiple_of(h * slab, slab), slab), :]
    for d in range(1, H):
        inner = inner + inner_r[d - 1]
    for e in range(E):
        w_v[pl.ds(e * slab, slab), :] = inner * (ids_v[...] == e).astype(F32)

    def combine(*accs):
        o = jnp.concatenate([o_hi, o_lo], axis=0)
        for unit, w in enumerate(split(w_v[...])):
            for j in range(0, tokens, TILE):
                slot = j // TILE % 2
                pltpu.matmul_push_rhs(o[:, j:j + TILE], slot, unit, transpose=True)
                pltpu.matmul_acc_lhs(accs[unit], w[:, j:j + TILE], slot)
        r = pltpu.matmul_pop(accs[0]) + pltpu.matmul_pop(accs[1])
        r_v[...] = r[:, :2 * width] + r[:, 2 * width:]

    pl.run_scoped(combine, *[pltpu.ACC(u)((E * slab, TILE), F32) for u in (0, 1)])
    left = lax.broadcasted_iota(jnp.int32, (E, 2 * width), 1) < width
    for n in range(half):
        y_v[n] = jnp.where(
            left, r_v[pl.ds(2 * n, E, stride=slab), :], r_v[pl.ds(2 * n + 1, E, stride=slab), :])

    def band(i):
        return pl.ds(i * part, part)

    send = []
    for d in range(1, A):
        pa = lax.rem(a + d, A)
        cp = pltpu.make_async_remote_copy(
            y_v.at[band(pa)], rs_r.at[d - 1], as_sem, ar_sem,
            device_id=(b * A + pa, h), device_id_type=MESH)
        cp.start()
        send.append(cp)
    loads["p"].wait()
    M = p_v.shape[0]
    fill((p_hi, p_lo), p_v, (pl.ds(0, M), slice(None)))
    loads["q"].wait()
    fill((q_hi, q_lo), q_v, (slice(None), pl.ds(0, M)))
    f2_v[...] = jnp.zeros(f2_v.shape, F32)
    im2_v[...] = jnp.zeros(im2_v.shape, F32)
    mine = y_v[band(a)]
    every = pltpu.make_async_copy(rs_r, rs_r, ar_sem)
    every.wait()
    for d in range(1, A):
        mine = mine + rs_r[d - 1]
    if B > 1:
        own_v[...] = mine
    zsend = []
    for d in range(1, B):
        pb = lax.rem(b + d, B)
        cp = pltpu.make_async_remote_copy(
            own_v, z_v.at[b], zs_sem.at[d - 1], zr_sem.at[b],
            device_id=(pb * A + a, h), device_id_type=MESH)
        cp.start()
        zsend.append(cp)
    if B > 1:
        z_v[b] = mine
    for d in range(1, B):
        pb = lax.rem(b + d, B)
        pltpu.make_async_remote_copy(
            own_v, z_v.at[pb], zs_sem.at[d - 1], zr_sem.at[pb],
            device_id=(pb * A + a, h), device_id_type=MESH).wait_recv()
    total = z_v[0] if B > 1 else mine
    for i in range(1, B):
        total = total + z_v[i]
    full_v[band(a)] = total
    G = min(4, A)
    ag, ai = lax.div(a, G), lax.rem(a, G)

    def gather(dg, di):
        pg = lax.rem(ag + dg, A // G)
        pa = pg * G + lax.rem(ai + di, G)
        return pltpu.make_async_remote_copy(
            full_v.at[band(a)], full_v.at[band(a)], gs_sem, gr_sem.at[ag],
            device_id=(b * A + pa, h), device_id_type=MESH)

    far = sorted(range(A // G), key=lambda g: -min(g, A // G - g))
    for dg in far[::-1]:
        for di in range(G):
            if dg or di:
                gather(dg, di).start()
    lanes = 2 * width
    gp = G * part
    groups = far[::-1]
    cuts = gp * lanes // TILE
    Q = q_hi.shape[0]
    tiles = Q // 128

    def score(im_hi, im_lo, *outs):
        rows = []
        for dg in groups:
            pg = lax.rem(ag + dg, A // G)
            for j in range(cuts):
                rows.append(pl.ds(pl.multiple_of(pg * (gp * lanes) + j * TILE, TILE), TILE))

        def push(n):
            for unit, p in enumerate((p_hi, p_lo)):
                pltpu.matmul_push_rhs(p[:, rows[n]], n % 2, unit, transpose=True)

        def push_q(n):
            for slot, q in enumerate((q_hi, q_lo)):
                pltpu.matmul_push_rhs(q[pl.ds(n * TILE, TILE), :], slot, n % 2, transpose=True)

        for n in range(min(2, len(rows))):
            push(n)
        step = 0
        for dg in groups:
            pg = lax.rem(ag + dg, A // G)
            n = gp if dg else gp - part
            if n:
                got = full_v.at[pl.ds(0, n)]
                pltpu.make_async_copy(got, got, gr_sem.at[pg]).wait()
            f = jnp.concatenate([full_v[pg * gp + i] for i in range(gp)], axis=1)
            f2_v[dg, pl.ds(0, E), :] = f
            f2_v[dg, pl.ds(E, E), :] = f - f.astype(BF).astype(F32)
            fb = f2_v[dg].astype(BF)
            for j in range(cuts):
                for acc in (im_hi, im_lo):
                    pltpu.matmul_acc_lhs(acc, fb[:, j * TILE:(j + 1) * TILE], step % 2)
                if step + 2 < len(rows):
                    push(step + 2)
                step += 1
        for n in range(min(2, Q // TILE)):
            push_q(n)
        im = pltpu.matmul_pop(im_hi) + pltpu.matmul_pop(im_lo)
        im = im[:E, :M] + im[E:2 * E, :M]
        im2_v[pl.ds(0, E), pl.ds(0, M)] = im
        im2_v[pl.ds(E, E), pl.ds(0, M)] = im - im.astype(BF).astype(F32)
        ib = im2_v[...].astype(BF)
        for n in range(Q // TILE):
            for slot in range(2):
                pltpu.matmul_acc_lhs(outs[n], ib, slot)
            if n + 2 < Q // TILE:
                push_q(n + 2)
        for n in range(Q // TILE):
            sc = pltpu.matmul_pop(outs[n])
            sc = sc[:E] + sc[E:2 * E]
            for i in range(TILE // 128):
                sc_v[n * (TILE // 128) + i] = sc[:, i * 128:(i + 1) * 128]

    tall = im2_v.shape[0]
    pl.run_scoped(
        score,
        *[pltpu.ACC(u)((tall, TILE), F32) for u in (0, 1)],
        *[pltpu.ACC(n % 2)((tall, TILE), F32) for n in range(Q // TILE)])
    per = T // tiles
    me = t * H + h

    def ssend(d):
        pt = lax.rem(t + lax.rem(d, T), T)
        ph = lax.rem(h + lax.div(d, T), H)
        return pltpu.make_async_remote_copy(
            sc_v.at[lax.div(pt, per)], s_v.at[me], ss_sem, sr_sem,
            device_id=(pt, ph), device_id_type=MESH)

    def loop(fn):
        lax.fori_loop(1, T * H, lambda d, c: (fn(d), c)[1], 0, unroll=T * H <= 32)

    loop(lambda d: ssend(d).start())
    s_v[me] = sc_v[lax.div(t, per)]
    for cp in hid_out + hid_in + zsend:
        cp.wait_send()
    for n in range(half):
        feats_out[:, pl.ds(n * lanes, lanes)] = full_v[n]
    got = s_v.at[pl.ds(0, T * H - 1)]
    pltpu.make_async_copy(got, got, sr_sem).wait()
    if T * H <= 32:
        parts = [s_v[i] for i in range(T * H)]
        while len(parts) > 1:
            parts = [parts[i] + parts[i + 1] for i in range(0, len(parts), 2)]
        tot = parts[0]
    else:
        tot = lax.fori_loop(0, T * H, lambda i, c: c + s_v[i], jnp.zeros(s_v.shape[1:], F32))
    span = 128 // per
    place = lax.rem(t, per)
    res = tot[:, :span]
    for i in range(1, per):
        res = jnp.where(place == i, tot[:, i * span:(i + 1) * span], res)
    scores_out[...] = res
    pltpu.make_async_copy(got, got, ss_sem).wait()
    pltpu.make_async_copy(rs_r, rs_r, as_sem).wait()
    got = full_v.at[pl.ds(0, half - part)]
    pltpu.make_async_copy(got, got, gs_sem).wait()


def finish(scores, feats, scores_out, feats_out):
    scores_out[...] = scores[...]
    feats_out[...] = feats[...]


def on_device(T, H, acts, out_grads, proj_in, proj_out, example_ids, queries, precond):
    tokens = acts.shape[0]
    E = 2 * tokens * T // EX_LEN
    width = proj_in.shape[1]
    slab = width // H
    half = slab // 2
    A = min(T, half)
    B = T // A
    part = half // A
    lanes = 2 * width
    cols = slab * width
    Q, M = queries.shape
    ci, co = 14, 4
    tall = -(-2 * E // 16) * 16
    D = pltpu.SemaphoreType.DMA
    V = pltpu.VMEM
    hbm = pl.BlockSpec(memory_space=pl.ANY)
    scores, feats = pl.pallas_call(
        functools.partial(kernel, T, H, A, E, ci, co),
        out_shape=(
            jax.ShapeDtypeStruct((E, Q // T), F32),
            jax.ShapeDtypeStruct((E, cols), F32),
        ),
        in_specs=[hbm] * 7,
        out_specs=(pl.BlockSpec(memory_space=pltpu.VMEM),) * 2,
        scratch_shapes=[
            V(acts.shape, BF), V(out_grads.shape, BF),
            V(proj_in.shape[::-1], BF), V(proj_out.shape[::-1], BF),
            V((1, tokens), jnp.int32), V((Q, M), F32), V(precond.shape, F32),
            V((Q, TILE), BF), V((Q, TILE), BF),
            V((TILE, precond.shape[1]), BF), V((TILE, precond.shape[1]), BF),
            V((width, tokens), F32), V((width, tokens), F32),
            V((H - 1, slab, tokens), F32), V((H - 1, width, tokens), F32),
            V((E * slab, lanes), F32), V((E * slab, tokens), F32),
            V((half, E, lanes), F32), V((A - 1, part, E, lanes), F32),
            V((B, part, E, lanes), F32), V((part, E, lanes), F32),
            V((half, E, lanes), F32),
            V((A // min(4, A), tall, min(4, A) * part * lanes), F32), V((tall, TILE), F32),
            V((Q // 128, E, 128), F32), V((T * H, E, 128), F32),
            D((5 + co + 2 * ci,)), D, D((2, H - 1)), D((2, H - 1)),
            D, D, D((max(B - 1, 1),)), D((B,)), D, D((A // min(4, A),)),
            D, D,
        ],
        compiler_params=pltpu.CompilerParams(
            collective_id=0, has_side_effects=True, vmem_limit_bytes=60000 * 1024
        ),
    )(acts, out_grads, proj_in.T, proj_out.T, example_ids.reshape(1, tokens), queries, precond)
    scores, feats = pl.pallas_call(
        finish,
        out_shape=(
            jax.ShapeDtypeStruct(scores.shape, F32),
            jax.ShapeDtypeStruct(feats.shape, F32),
        ),
    )(scores, feats)
    return scores.T, feats


def solution(mesh):
    T, H = mesh.shape["tok"], mesh.shape["hid"]
    in_specs = (
        P("tok", "hid"),
        P("tok", "hid"),
        P("hid", None),
        P("hid", None),
        P("tok"),
        P(None, "tok"),
        P("tok", "hid"),
    )
    out_specs = (P("tok", None), P(None, "hid"))
    return jax.shard_map(
        functools.partial(on_device, T, H), mesh=mesh, in_specs=in_specs, out_specs=out_specs,
        check_vma=False,
    )
```

```python
import functools

import jax
import jax.numpy as jnp
from jax import lax
from jax.experimental import pallas as pl
from jax.experimental.pallas import tpu as pltpu
from jax.sharding import PartitionSpec as P

EX_LEN = 2048
TILE = 256
MESH = pl.DeviceIdType.MESH
BF, F32 = jnp.bfloat16, jnp.float32


def split(x):
    hi = x.astype(BF)
    return hi, (x - hi.astype(F32)).astype(BF)


def fill(pair, src, at):
    for ref in pair:
        if ref.shape != src.shape:
            ref[...] = jnp.zeros(ref.shape, BF)
    for ref, half in zip(pair, split(src[...])):
        ref[at] = half


def kernel(
    T, H, A, E, ci, co,
    acts, grads, pin, pout, ids, queries, precond,
    scores_out, feats_out,
    acts_v, grads_v, pin_v, pout_v, ids_v, q_v, p_v,
    q_hi, q_lo, p_hi, p_lo,
    inner_v, outer_v, inner_r, outer_r, r_v, w_v, y_v, rs_r, z_v, own_v, full_v,
    f2_v, im2_v, sc_v, s_v,
    ld_sem, in_sem, hs_sem, hr_sem, as_sem, ar_sem, zs_sem, zr_sem, gs_sem, gr_sem,
    ss_sem, sr_sem,
):
    B = T // A
    t, h = lax.axis_index("tok"), lax.axis_index("hid")
    a, b = lax.rem(t, A), lax.div(t, A)
    width, tokens = inner_v.shape
    slab = width // H
    half = slab // 2
    part = half // A

    loads = {}

    def load(name, src, dst):
        c = pltpu.make_async_copy(src, dst, ld_sem.at[len(loads)])
        c.start()
        loads[name] = c

    load("pout", pout, pout_v)
    go = grads.shape[1] // co
    for c in range(co):
        k = pl.ds(c * go, go)
        load(("g", c), grads.at[:, k], grads_v.at[:, k])
    gi = acts.shape[1] // ci
    for c in range(ci):
        k = pl.ds(c * gi, gi)
        load(("pi", c), pin.at[:, k], pin_v.at[:, k])
        load(("a", c), acts.at[:, k], acts_v.at[:, k])
    load("ids", ids, ids_v)
    load("p", precond, p_v)
    load("q", queries, q_v)

    def peer(d):
        return lax.rem(t + d // H, T), lax.rem(h + d % H, H)

    barrier = pltpu.get_barrier_semaphore()
    everyone = T * H - 1

    def greet(d, _):
        pt = lax.rem(t + lax.div(d, H), T)
        ph = lax.rem(h + lax.rem(d, H), H)
        pl.semaphore_signal(barrier, inc=1, device_id=(pt, ph), device_id_type=MESH)
        return 0

    lax.fori_loop(1, T * H, greet, 0, unroll=T * H <= 32)

    hid_out, hid_in = [], []
    for d in range(1, H):
        hid_out.append(pltpu.make_async_remote_copy(
            outer_v, outer_r.at[d - 1], hs_sem.at[0, d - 1], hr_sem.at[0, d - 1],
            device_id=(t, lax.rem(h + d, H)), device_id_type=MESH))

    def project(*accs):
        step = 0

        def tiles(x, y, start, size, pair):
            nonlocal step
            for j in range(0, size, TILE):
                k = pl.ds(start + j, TILE)
                unit, slot = step % 2, step // 2 % 2
                pltpu.matmul_push_rhs(y[:, k], slot, unit, transpose=True)
                pltpu.matmul_acc_lhs(pair[unit], x[:, k], slot)
                step += 1

        loads["pout"].wait()
        for c in range(co):
            loads[("g", c)].wait()
            tiles(pout_v, grads_v, c * go, go, accs[:2])
        outer_v[...] = pltpu.matmul_pop(accs[0]) + pltpu.matmul_pop(accs[1])
        for c in range(ci):
            if c == ci - 1:
                pl.semaphore_wait(barrier, everyone)
                for cp in hid_out:
                    cp.start()
            loads[("pi", c)].wait()
            loads[("a", c)].wait()
            tiles(pin_v, acts_v, c * gi, gi, accs[2:])
        inner_v[...] = pltpu.matmul_pop(accs[2]) + pltpu.matmul_pop(accs[3])

    pl.run_scoped(project, *[pltpu.ACC(u)((width, tokens), F32) for u in (0, 1, 0, 1)])
    for d in range(1, H):
        ph = lax.rem(h + d, H)
        cp = pltpu.make_async_remote_copy(
            inner_v.at[pl.ds(pl.multiple_of(ph * slab, slab), slab), :], inner_r.at[d - 1],
            hs_sem.at[1, d - 1], hr_sem.at[1, d - 1],
            device_id=(t, ph), device_id_type=MESH)
        cp.start()
        hid_in.append(cp)
    loads["ids"].wait()

    for cp in hid_out:
        cp.wait_recv()
    outer = outer_v[...]
    for d in range(1, H):
        outer = outer + outer_r[d - 1]
    o_hi, o_lo = split(jnp.concatenate([outer, outer], axis=0))
    for cp in hid_in:
        cp.wait_recv()
    inner = inner_v[pl.ds(pl.multiple_of(h * slab, slab), slab), :]
    for d in range(1, H):
        inner = inner + inner_r[d - 1]
    for e in range(E):
        w_v[pl.ds(e * slab, slab), :] = inner * (ids_v[...] == e).astype(F32)

    def combine(*accs):
        o = jnp.concatenate([o_hi, o_lo], axis=0)
        for unit, w in enumerate(split(w_v[...])):
            for j in range(0, tokens, TILE):
                slot = j // TILE % 2
                pltpu.matmul_push_rhs(o[:, j:j + TILE], slot, unit, transpose=True)
                pltpu.matmul_acc_lhs(accs[unit], w[:, j:j + TILE], slot)
        r = pltpu.matmul_pop(accs[0]) + pltpu.matmul_pop(accs[1])
        r_v[...] = r[:, :2 * width] + r[:, 2 * width:]

    pl.run_scoped(combine, *[pltpu.ACC(u)((E * slab, TILE), F32) for u in (0, 1)])
    left = lax.broadcasted_iota(jnp.int32, (E, 2 * width), 1) < width
    for n in range(half):
        y_v[n] = jnp.where(
            left, r_v[pl.ds(2 * n, E, stride=slab), :], r_v[pl.ds(2 * n + 1, E, stride=slab), :])

    def band(i):
        return pl.ds(i * part, part)

    send = []
    for d in range(1, A):
        pa = lax.rem(a + d, A)
        cp = pltpu.make_async_remote_copy(
            y_v.at[band(pa)], rs_r.at[d - 1], as_sem, ar_sem,
            device_id=(b * A + pa, h), device_id_type=MESH)
        cp.start()
        send.append(cp)
    loads["p"].wait()
    M = p_v.shape[0]
    fill((p_hi, p_lo), p_v, (pl.ds(0, M), slice(None)))
    loads["q"].wait()
    fill((q_hi, q_lo), q_v, (slice(None), pl.ds(0, M)))
    f2_v[...] = jnp.zeros(f2_v.shape, F32)
    im2_v[...] = jnp.zeros(im2_v.shape, F32)
    mine = y_v[band(a)]
    every = pltpu.make_async_copy(rs_r, rs_r, ar_sem)
    every.wait()
    for d in range(1, A):
        mine = mine + rs_r[d - 1]
    if B > 1:
        own_v[...] = mine
    zsend = []
    for d in range(1, B):
        pb = lax.rem(b + d, B)
        cp = pltpu.make_async_remote_copy(
            own_v, z_v.at[b], zs_sem.at[d - 1], zr_sem.at[b],
            device_id=(pb * A + a, h), device_id_type=MESH)
        cp.start()
        zsend.append(cp)
    if B > 1:
        z_v[b] = mine
    for d in range(1, B):
        pb = lax.rem(b + d, B)
        pltpu.make_async_remote_copy(
            own_v, z_v.at[pb], zs_sem.at[d - 1], zr_sem.at[pb],
            device_id=(pb * A + a, h), device_id_type=MESH).wait_recv()
    total = z_v[0] if B > 1 else mine
    for i in range(1, B):
        total = total + z_v[i]
    full_v[band(a)] = total
    G = min(4, A)
    ag, ai = lax.div(a, G), lax.rem(a, G)

    def gather(dg, di):
        pg = lax.rem(ag + dg, A // G)
        pa = pg * G + lax.rem(ai + di, G)
        return pltpu.make_async_remote_copy(
            full_v.at[band(a)], full_v.at[band(a)], gs_sem, gr_sem.at[ag],
            device_id=(b * A + pa, h), device_id_type=MESH)

    far = sorted(range(A // G), key=lambda g: -min(g, A // G - g))
    for dg in far[::-1]:
        for di in range(G):
            if dg or di:
                gather(dg, di).start()
    lanes = 2 * width
    gp = G * part
    groups = far[::-1]
    cuts = gp * lanes // TILE
    Q = q_hi.shape[0]
    tiles = Q // 128

    def score(im_hi, im_lo, *outs):
        rows = []
        for dg in groups:
            pg = lax.rem(ag + dg, A // G)
            for j in range(cuts):
                rows.append(pl.ds(pl.multiple_of(pg * (gp * lanes) + j * TILE, TILE), TILE))

        def push(n):
            for unit, p in enumerate((p_hi, p_lo)):
                pltpu.matmul_push_rhs(p[:, rows[n]], n % 2, unit, transpose=True)

        def push_q(n):
            for slot, q in enumerate((q_hi, q_lo)):
                pltpu.matmul_push_rhs(q[pl.ds(n * TILE, TILE), :], slot, n % 2, transpose=True)

        for n in range(min(2, len(rows))):
            push(n)
        step = 0
        for dg in groups:
            pg = lax.rem(ag + dg, A // G)
            n = gp if dg else gp - part
            if n:
                got = full_v.at[pl.ds(0, n)]
                pltpu.make_async_copy(got, got, gr_sem.at[pg]).wait()
            f = jnp.concatenate([full_v[pg * gp + i] for i in range(gp)], axis=1)
            f2_v[dg, pl.ds(0, E), :] = f
            f2_v[dg, pl.ds(E, E), :] = f - f.astype(BF).astype(F32)
            fb = f2_v[dg].astype(BF)
            for j in range(cuts):
                for acc in (im_hi, im_lo):
                    pltpu.matmul_acc_lhs(acc, fb[:, j * TILE:(j + 1) * TILE], step % 2)
                if step + 2 < len(rows):
                    push(step + 2)
                step += 1
        for n in range(min(2, Q // TILE)):
            push_q(n)
        im = pltpu.matmul_pop(im_hi) + pltpu.matmul_pop(im_lo)
        im = im[:E, :M] + im[E:2 * E, :M]
        im2_v[pl.ds(0, E), pl.ds(0, M)] = im
        im2_v[pl.ds(E, E), pl.ds(0, M)] = im - im.astype(BF).astype(F32)
        ib = im2_v[...].astype(BF)
        for n in range(Q // TILE):
            for slot in range(2):
                pltpu.matmul_acc_lhs(outs[n], ib, slot)
            if n + 2 < Q // TILE:
                push_q(n + 2)
        for n in range(Q // TILE):
            sc = pltpu.matmul_pop(outs[n])
            sc = sc[:E] + sc[E:2 * E]
            for i in range(TILE // 128):
                sc_v[n * (TILE // 128) + i] = sc[:, i * 128:(i + 1) * 128]

    tall = im2_v.shape[0]
    pl.run_scoped(
        score,
        *[pltpu.ACC(u)((tall, TILE), F32) for u in (0, 1)],
        *[pltpu.ACC(n % 2)((tall, TILE), F32) for n in range(Q // TILE)])
    per = T // tiles
    me = t * H + h

    def ssend(d):
        pt = lax.rem(t + lax.rem(d, T), T)
        ph = lax.rem(h + lax.div(d, T), H)
        return pltpu.make_async_remote_copy(
            sc_v.at[lax.div(pt, per)], s_v.at[me], ss_sem, sr_sem,
            device_id=(pt, ph), device_id_type=MESH)

    def loop(fn):
        lax.fori_loop(1, T * H, lambda d, c: (fn(d), c)[1], 0, unroll=T * H <= 32)

    loop(lambda d: ssend(d).start())
    s_v[me] = sc_v[lax.div(t, per)]
    for cp in hid_out + hid_in + zsend:
        cp.wait_send()
    for n in range(half):
        feats_out[:, pl.ds(n * lanes, lanes)] = full_v[n]
    got = s_v.at[pl.ds(0, T * H - 1)]
    pltpu.make_async_copy(got, got, sr_sem).wait()
    if T * H <= 32:
        parts = [s_v[i] for i in range(T * H)]
        while len(parts) > 1:
            parts = [parts[i] + parts[i + 1] for i in range(0, len(parts), 2)]
        tot = parts[0]
    else:
        tot = lax.fori_loop(0, T * H, lambda i, c: c + s_v[i], jnp.zeros(s_v.shape[1:], F32))
    span = 128 // per
    place = lax.rem(t, per)
    res = tot[:, :span]
    for i in range(1, per):
        res = jnp.where(place == i, tot[:, i * span:(i + 1) * span], res)
    scores_out[...] = res
    pltpu.make_async_copy(got, got, ss_sem).wait()
    pltpu.make_async_copy(rs_r, rs_r, as_sem).wait()
    got = full_v.at[pl.ds(0, half - part)]
    pltpu.make_async_copy(got, got, gs_sem).wait()


def finish(scores, feats, scores_out, feats_out):
    scores_out[...] = scores[...]
    feats_out[...] = feats[...]


def on_device(T, H, acts, out_grads, proj_in, proj_out, example_ids, queries, precond):
    tokens = acts.shape[0]
    E = 2 * tokens * T // EX_LEN
    width = proj_in.shape[1]
    slab = width // H
    half = slab // 2
    A = min(T, half)
    B = T // A
    part = half // A
    lanes = 2 * width
    cols = slab * width
    Q, M = queries.shape
    ci, co = 14, 4
    tall = -(-2 * E // 16) * 16
    D = pltpu.SemaphoreType.DMA
    V = pltpu.VMEM
    hbm = pl.BlockSpec(memory_space=pltpu.HBM)
    scores, feats = pl.pallas_call(
        functools.partial(kernel, T, H, A, E, ci, co),
        out_shape=(
            jax.ShapeDtypeStruct((E, Q // T), F32),
            jax.ShapeDtypeStruct((E, cols), F32),
        ),
        in_specs=[hbm] * 7,
        out_specs=(pl.BlockSpec(memory_space=pltpu.VMEM),) * 2,
        scratch_shapes=[
            V(acts.shape, BF), V(out_grads.shape, BF),
            V(proj_in.shape[::-1], BF), V(proj_out.shape[::-1], BF),
            V((1, tokens), jnp.int32), V((Q, M), F32), V(precond.shape, F32),
            V((Q, TILE), BF), V((Q, TILE), BF),
            V((TILE, precond.shape[1]), BF), V((TILE, precond.shape[1]), BF),
            V((width, tokens), F32), V((width, tokens), F32),
            V((H - 1, slab, tokens), F32), V((H - 1, width, tokens), F32),
            V((E * slab, lanes), F32), V((E * slab, tokens), F32),
            V((half, E, lanes), F32), V((A - 1, part, E, lanes), F32),
            V((B, part, E, lanes), F32), V((part, E, lanes), F32),
            V((half, E, lanes), F32),
            V((A // min(4, A), tall, min(4, A) * part * lanes), F32), V((tall, TILE), F32),
            V((Q // 128, E, 128), F32), V((T * H, E, 128), F32),
            D((5 + co + 2 * ci,)), D, D((2, H - 1)), D((2, H - 1)),
            D, D, D((max(B - 1, 1),)), D((B,)), D, D((A // min(4, A),)),
            D, D,
        ],
        compiler_params=pltpu.CompilerParams(
            collective_id=0, has_side_effects=True, vmem_limit_bytes=32000 * 1024
        ),
    )(*[pltpu.with_memory_space_constraint(x, pltpu.HBM) for x in (
        acts, out_grads, proj_in.T, proj_out.T, example_ids.reshape(1, tokens), queries, precond)])
    scores, feats = pl.pallas_call(
        finish,
        out_shape=(
            jax.ShapeDtypeStruct(scores.shape, F32),
            jax.ShapeDtypeStruct(feats.shape, F32),
        ),
        compiler_params=pltpu.CompilerParams(vmem_limit_bytes=1024 * 1024),
    )(scores, feats)
    return scores.T, feats


def solution(mesh):
    T, H = mesh.shape["tok"], mesh.shape["hid"]
    in_specs = (
        P("tok", "hid"),
        P("tok", "hid"),
        P("hid", None),
        P("hid", None),
        P("tok"),
        P(None, "tok"),
        P("tok", "hid"),
    )
    out_specs = (P("tok", None), P(None, "hid"))
    return jax.shard_map(
        functools.partial(on_device, T, H), mesh=mesh, in_specs=in_specs, out_specs=out_specs,
        check_vma=False,
    )
```

```python
import functools

import jax
import jax.numpy as jnp
from jax import lax
from jax.experimental import pallas as pl
from jax.experimental.pallas import tpu as pltpu
from jax.sharding import PartitionSpec as P

EX_LEN = 2048
TILE = 256
MESH = pl.DeviceIdType.MESH
BF, F32 = jnp.bfloat16, jnp.float32


def split(x):
    hi = x.astype(BF)
    return hi, (x - hi.astype(F32)).astype(BF)


def fill(pair, src, at):
    for ref in pair:
        if ref.shape != src.shape:
            ref[...] = jnp.zeros(ref.shape, BF)
    for ref, half in zip(pair, split(src[...])):
        ref[at] = half


def kernel(
    T, H, A, E, ci, co,
    acts, grads, pin, pout, ids, queries, precond,
    scores_out, feats_out,
    acts_v, grads_v, pin_v, pout_v, ids_v, q_v, p_v,
    q_hi, q_lo, p_hi, p_lo,
    inner_v, outer_v, inner_r, outer_r, r_v, w_v, y_v, rs_r, all_v, full_v,
    f2_v, im2_v, sc_v, s_v,
    ld_sem, in_sem, hs_sem, hr_sem, as_sem, ar_sem, gs_sem, gr_sem,
    ss_sem, sr_sem,
):
    B = T // A
    t, h = lax.axis_index("tok"), lax.axis_index("hid")
    a, b = lax.rem(t, A), lax.div(t, A)
    width, tokens = inner_v.shape
    slab = width // H
    half = slab // 2
    part = half // A

    loads = {}

    def load(name, src, dst):
        c = pltpu.make_async_copy(src, dst, ld_sem.at[len(loads)])
        c.start()
        loads[name] = c

    load("pout", pout, pout_v)
    go = grads.shape[1] // co
    for c in range(co):
        k = pl.ds(c * go, go)
        load(("g", c), grads.at[:, k], grads_v.at[:, k])
    gi = acts.shape[1] // ci
    for c in range(ci):
        k = pl.ds(c * gi, gi)
        load(("pi", c), pin.at[:, k], pin_v.at[:, k])
        load(("a", c), acts.at[:, k], acts_v.at[:, k])
    load("ids", ids, ids_v)
    load("p", precond, p_v)
    load("q", queries, q_v)

    def peer(d):
        return lax.rem(t + d // H, T), lax.rem(h + d % H, H)

    barrier = pltpu.get_barrier_semaphore()
    everyone = T * H - 1

    def greet(d, _):
        pt = lax.rem(t + lax.div(d, H), T)
        ph = lax.rem(h + lax.rem(d, H), H)
        pl.semaphore_signal(barrier, inc=1, device_id=(pt, ph), device_id_type=MESH)
        return 0

    lax.fori_loop(1, T * H, greet, 0, unroll=T * H <= 32)

    hid_out, hid_in = [], []
    for d in range(1, H):
        hid_out.append(pltpu.make_async_remote_copy(
            outer_v, outer_r.at[d - 1], hs_sem.at[0, d - 1], hr_sem.at[0, d - 1],
            device_id=(t, lax.rem(h + d, H)), device_id_type=MESH))

    def project(*accs):
        step = 0

        def tiles(x, y, start, size, pair):
            nonlocal step
            for j in range(0, size, TILE):
                k = pl.ds(start + j, TILE)
                unit, slot = step % 2, step // 2 % 2
                pltpu.matmul_push_rhs(y[:, k], slot, unit, transpose=True)
                pltpu.matmul_acc_lhs(pair[unit], x[:, k], slot)
                step += 1

        loads["pout"].wait()
        for c in range(co):
            loads[("g", c)].wait()
            tiles(pout_v, grads_v, c * go, go, accs[:2])
        outer_v[...] = pltpu.matmul_pop(accs[0]) + pltpu.matmul_pop(accs[1])
        for c in range(ci):
            if c == ci - 1:
                pl.semaphore_wait(barrier, everyone)
                for cp in hid_out:
                    cp.start()
            loads[("pi", c)].wait()
            loads[("a", c)].wait()
            tiles(pin_v, acts_v, c * gi, gi, accs[2:])
        inner_v[...] = pltpu.matmul_pop(accs[2]) + pltpu.matmul_pop(accs[3])

    pl.run_scoped(project, *[pltpu.ACC(u)((width, tokens), F32) for u in (0, 1, 0, 1)])
    for d in range(1, H):
        ph = lax.rem(h + d, H)
        cp = pltpu.make_async_remote_copy(
            inner_v.at[pl.ds(pl.multiple_of(ph * slab, slab), slab), :], inner_r.at[d - 1],
            hs_sem.at[1, d - 1], hr_sem.at[1, d - 1],
            device_id=(t, ph), device_id_type=MESH)
        cp.start()
        hid_in.append(cp)
    loads["ids"].wait()

    for cp in hid_out:
        cp.wait_recv()
    outer = outer_v[...]
    for d in range(1, H):
        outer = outer + outer_r[d - 1]
    o_hi, o_lo = split(jnp.concatenate([outer, outer], axis=0))
    for cp in hid_in:
        cp.wait_recv()
    inner = inner_v[pl.ds(pl.multiple_of(h * slab, slab), slab), :]
    for d in range(1, H):
        inner = inner + inner_r[d - 1]
    for e in range(E):
        w_v[pl.ds(e * slab, slab), :] = inner * (ids_v[...] == e).astype(F32)

    def combine(*accs):
        o = jnp.concatenate([o_hi, o_lo], axis=0)
        for unit, w in enumerate(split(w_v[...])):
            for j in range(0, tokens, TILE):
                slot = j // TILE % 2
                pltpu.matmul_push_rhs(o[:, j:j + TILE], slot, unit, transpose=True)
                pltpu.matmul_acc_lhs(accs[unit], w[:, j:j + TILE], slot)
        r = pltpu.matmul_pop(accs[0]) + pltpu.matmul_pop(accs[1])
        r_v[...] = r[:, :2 * width] + r[:, 2 * width:]

    pl.run_scoped(combine, *[pltpu.ACC(u)((E * slab, TILE), F32) for u in (0, 1)])
    left = lax.broadcasted_iota(jnp.int32, (E, 2 * width), 1) < width
    for n in range(half):
        y_v[n] = jnp.where(
            left, r_v[pl.ds(2 * n, E, stride=slab), :], r_v[pl.ds(2 * n + 1, E, stride=slab), :])

    def band(i):
        return pl.ds(i * part, part)

    send = []
    for d in range(1, A):
        pa = lax.rem(a + d, A)
        cp = pltpu.make_async_remote_copy(
            y_v.at[band(pa)], rs_r.at[d - 1], as_sem, ar_sem,
            device_id=(b * A + pa, h), device_id_type=MESH)
        cp.start()
        send.append(cp)
    loads["p"].wait()
    M = p_v.shape[0]
    fill((p_hi, p_lo), p_v, (pl.ds(0, M), slice(None)))
    loads["q"].wait()
    fill((q_hi, q_lo), q_v, (slice(None), pl.ds(0, M)))
    f2_v[...] = jnp.zeros(f2_v.shape, F32)
    im2_v[...] = jnp.zeros(im2_v.shape, F32)
    mine = y_v[band(a)]
    every = pltpu.make_async_copy(rs_r, rs_r, ar_sem)
    every.wait()
    for d in range(1, A):
        mine = mine + rs_r[d - 1]
    all_v[b, band(a)] = mine

    def gather(db, da):
        pb, pa = lax.rem(b + db, B), lax.rem(a + da, A)
        return pltpu.make_async_remote_copy(
            all_v.at[b, band(a)], all_v.at[b, band(a)], gs_sem, gr_sem.at[b],
            device_id=(pb * A + pa, h), device_id_type=MESH)

    for db in sorted(range(B), key=lambda g: -min(g, B - g)):
        for da in range(A)[::-1]:
            if db or da:
                gather(db, da).start()
    for db in range(B):
        got = all_v.at[0, pl.ds(0, half if db else half - part)]
        pltpu.make_async_copy(got, got, gr_sem.at[lax.rem(b + db, B)]).wait()
    total = all_v[0]
    for i in range(1, B):
        total = total + all_v[i]
    full_v[...] = total
    lanes = 2 * width
    cuts = half * lanes // TILE
    Q = q_hi.shape[0]
    tiles = Q // 128

    def score(im_hi, im_lo, *outs):
        rows = [pl.ds(j * TILE, TILE) for j in range(cuts)]

        def push(n):
            for unit, p in enumerate((p_hi, p_lo)):
                pltpu.matmul_push_rhs(p[:, rows[n]], n % 2, unit, transpose=True)

        def push_q(n):
            for slot, q in enumerate((q_hi, q_lo)):
                pltpu.matmul_push_rhs(q[pl.ds(n * TILE, TILE), :], slot, n % 2, transpose=True)

        for n in range(min(2, len(rows))):
            push(n)
        f = jnp.concatenate([full_v[i] for i in range(half)], axis=1)
        f2_v[pl.ds(0, E), :] = f
        f2_v[pl.ds(E, E), :] = f - f.astype(BF).astype(F32)
        fb = f2_v[...].astype(BF)
        for j in range(cuts):
            for acc in (im_hi, im_lo):
                pltpu.matmul_acc_lhs(acc, fb[:, j * TILE:(j + 1) * TILE], j % 2)
            if j + 2 < cuts:
                push(j + 2)
        for n in range(min(2, Q // TILE)):
            push_q(n)
        im = pltpu.matmul_pop(im_hi) + pltpu.matmul_pop(im_lo)
        im = im[:E, :M] + im[E:2 * E, :M]
        im2_v[pl.ds(0, E), pl.ds(0, M)] = im
        im2_v[pl.ds(E, E), pl.ds(0, M)] = im - im.astype(BF).astype(F32)
        ib = im2_v[...].astype(BF)
        for n in range(Q // TILE):
            for slot in range(2):
                pltpu.matmul_acc_lhs(outs[n], ib, slot)
            if n + 2 < Q // TILE:
                push_q(n + 2)
        for n in range(Q // TILE):
            sc = pltpu.matmul_pop(outs[n])
            sc = sc[:E] + sc[E:2 * E]
            for i in range(TILE // 128):
                sc_v[n * (TILE // 128) + i] = sc[:, i * 128:(i + 1) * 128]

    tall = im2_v.shape[0]
    pl.run_scoped(
        score,
        *[pltpu.ACC(u)((tall, TILE), F32) for u in (0, 1)],
        *[pltpu.ACC(n % 2)((tall, TILE), F32) for n in range(Q // TILE)])
    per = T // tiles
    me = t * H + h

    def ssend(d):
        pt = lax.rem(t + lax.rem(d, T), T)
        ph = lax.rem(h + lax.div(d, T), H)
        return pltpu.make_async_remote_copy(
            sc_v.at[lax.div(pt, per)], s_v.at[me], ss_sem, sr_sem,
            device_id=(pt, ph), device_id_type=MESH)

    def loop(fn):
        lax.fori_loop(1, T * H, lambda d, c: (fn(d), c)[1], 0, unroll=T * H <= 32)

    loop(lambda d: ssend(d).start())
    s_v[me] = sc_v[lax.div(t, per)]
    for cp in hid_out + hid_in:
        cp.wait_send()
    for n in range(half):
        feats_out[:, pl.ds(n * lanes, lanes)] = full_v[n]
    got = s_v.at[pl.ds(0, T * H - 1)]
    pltpu.make_async_copy(got, got, sr_sem).wait()
    if T * H <= 32:
        parts = [s_v[i] for i in range(T * H)]
        while len(parts) > 1:
            parts = [parts[i] + parts[i + 1] for i in range(0, len(parts), 2)]
        tot = parts[0]
    else:
        tot = lax.fori_loop(0, T * H, lambda i, c: c + s_v[i], jnp.zeros(s_v.shape[1:], F32))
    span = 128 // per
    place = lax.rem(t, per)
    res = tot[:, :span]
    for i in range(1, per):
        res = jnp.where(place == i, tot[:, i * span:(i + 1) * span], res)
    scores_out[...] = res
    pltpu.make_async_copy(got, got, ss_sem).wait()
    pltpu.make_async_copy(rs_r, rs_r, as_sem).wait()
    for n in [half] * (B - 1) + [half - part]:
        got = all_v.at[0, pl.ds(0, n)]
        pltpu.make_async_copy(got, got, gs_sem).wait()


def finish(scores, feats, scores_out, feats_out):
    scores_out[...] = scores[...]
    feats_out[...] = feats[...]


def on_device(T, H, acts, out_grads, proj_in, proj_out, example_ids, queries, precond):
    tokens = acts.shape[0]
    E = 2 * tokens * T // EX_LEN
    width = proj_in.shape[1]
    slab = width // H
    half = slab // 2
    A = min(T, half, 8)
    B = T // A
    part = half // A
    lanes = 2 * width
    cols = slab * width
    Q, M = queries.shape
    ci, co = 14, 4
    tall = -(-2 * E // 16) * 16
    D = pltpu.SemaphoreType.DMA
    V = pltpu.VMEM
    hbm = pl.BlockSpec(memory_space=pltpu.HBM)
    scores, feats = pl.pallas_call(
        functools.partial(kernel, T, H, A, E, ci, co),
        out_shape=(
            jax.ShapeDtypeStruct((E, Q // T), F32),
            jax.ShapeDtypeStruct((E, cols), F32),
        ),
        in_specs=[hbm] * 7,
        out_specs=(pl.BlockSpec(memory_space=pltpu.VMEM),) * 2,
        scratch_shapes=[
            V(acts.shape, BF), V(out_grads.shape, BF),
            V(proj_in.shape[::-1], BF), V(proj_out.shape[::-1], BF),
            V((1, tokens), jnp.int32), V((Q, M), F32), V(precond.shape, F32),
            V((Q, TILE), BF), V((Q, TILE), BF),
            V((TILE, precond.shape[1]), BF), V((TILE, precond.shape[1]), BF),
            V((width, tokens), F32), V((width, tokens), F32),
            V((H - 1, slab, tokens), F32), V((H - 1, width, tokens), F32),
            V((E * slab, lanes), F32), V((E * slab, tokens), F32),
            V((half, E, lanes), F32), V((A - 1, part, E, lanes), F32),
            V((B, half, E, lanes), F32), V((half, E, lanes), F32),
            V((tall, half * lanes), F32), V((tall, TILE), F32),
            V((Q // 128, E, 128), F32), V((T * H, E, 128), F32),
            D((5 + co + 2 * ci,)), D, D((2, H - 1)), D((2, H - 1)),
            D, D, D, D((B,)),
            D, D,
        ],
        compiler_params=pltpu.CompilerParams(
            collective_id=0, has_side_effects=True, vmem_limit_bytes=32000 * 1024
        ),
    )(*[pltpu.with_memory_space_constraint(x, pltpu.HBM) for x in (
        acts, out_grads, proj_in.T, proj_out.T, example_ids.reshape(1, tokens), queries, precond)])
    scores, feats = pl.pallas_call(
        finish,
        out_shape=(
            jax.ShapeDtypeStruct(scores.shape, F32),
            jax.ShapeDtypeStruct(feats.shape, F32),
        ),
        compiler_params=pltpu.CompilerParams(vmem_limit_bytes=1024 * 1024),
    )(scores, feats)
    return scores.T, feats


def solution(mesh):
    T, H = mesh.shape["tok"], mesh.shape["hid"]
    in_specs = (
        P("tok", "hid"),
        P("tok", "hid"),
        P("hid", None),
        P("hid", None),
        P("tok"),
        P(None, "tok"),
        P("tok", "hid"),
    )
    out_specs = (P("tok", None), P(None, "hid"))
    return jax.shard_map(
        functools.partial(on_device, T, H), mesh=mesh, in_specs=in_specs, out_specs=out_specs,
        check_vma=False,
    )
```

```python
import functools

import jax
import jax.numpy as jnp
from jax import lax
from jax.experimental import pallas as pl
from jax.experimental.pallas import tpu as pltpu
from jax.sharding import PartitionSpec as P

EX_LEN = 2048
TILE = 256
MESH = pl.DeviceIdType.MESH
BF, F32 = jnp.bfloat16, jnp.float32


def split(x):
    hi = x.astype(BF)
    return hi, (x - hi.astype(F32)).astype(BF)


def fill(pair, src, at):
    for ref in pair:
        if ref.shape != src.shape:
            ref[...] = jnp.zeros(ref.shape, BF)
    for ref, half in zip(pair, split(src[...])):
        ref[at] = half


def kernel(
    T, H, A, E, ci, co,
    acts, grads, pin, pout, ids, queries, precond,
    scores_out, feats_out,
    acts_v, grads_v, pin_v, pout_v, ids_v, q_v, p_v,
    q_hi, q_lo, p_hi, p_lo,
    inner_v, outer_v, inner_r, outer_r, r_v, w_v, y_v, rs_r, all_v, full_v,
    f2_v, im2_v, sc_v, s_v,
    ld_sem, in_sem, hs_sem, hr_sem, as_sem, ar_sem, gs_sem, gr_sem,
    ss_sem, sr_sem,
):
    B = T // A
    t, h = lax.axis_index("tok"), lax.axis_index("hid")
    a, b = lax.rem(t, A), lax.div(t, A)
    width, tokens = inner_v.shape
    slab = width // H
    half = slab // 2
    part = half // A

    loads = {}

    def load(name, src, dst):
        c = pltpu.make_async_copy(src, dst, ld_sem.at[len(loads)])
        c.start()
        loads[name] = c

    load("pout", pout, pout_v)
    go = grads.shape[1] // co
    for c in range(co):
        k = pl.ds(c * go, go)
        load(("g", c), grads.at[:, k], grads_v.at[:, k])
    gi = acts.shape[1] // ci
    for c in range(ci):
        k = pl.ds(c * gi, gi)
        load(("pi", c), pin.at[:, k], pin_v.at[:, k])
        load(("a", c), acts.at[:, k], acts_v.at[:, k])
    load("ids", ids, ids_v)
    load("p", precond, p_v)
    load("q", queries, q_v)

    def peer(d):
        return lax.rem(t + d // H, T), lax.rem(h + d % H, H)

    barrier = pltpu.get_barrier_semaphore()
    everyone = T * H - 1

    def greet(d, _):
        pt = lax.rem(t + lax.div(d, H), T)
        ph = lax.rem(h + lax.rem(d, H), H)
        pl.semaphore_signal(barrier, inc=1, device_id=(pt, ph), device_id_type=MESH)
        return 0

    lax.fori_loop(1, T * H, greet, 0, unroll=T * H <= 32)

    hid_out, hid_in = [], []
    for d in range(1, H):
        hid_out.append(pltpu.make_async_remote_copy(
            outer_v, outer_r.at[d - 1], hs_sem.at[0, d - 1], hr_sem.at[0, d - 1],
            device_id=(t, lax.rem(h + d, H)), device_id_type=MESH))

    def project(*accs):
        step = 0

        def tiles(x, y, start, size, pair):
            nonlocal step
            for j in range(0, size, TILE):
                k = pl.ds(start + j, TILE)
                unit, slot = step % 2, step // 2 % 2
                pltpu.matmul_push_rhs(y[:, k], slot, unit, transpose=True)
                pltpu.matmul_acc_lhs(pair[unit], x[:, k], slot)
                step += 1

        loads["pout"].wait()
        for c in range(co):
            loads[("g", c)].wait()
            tiles(pout_v, grads_v, c * go, go, accs[:2])
        outer_v[...] = pltpu.matmul_pop(accs[0]) + pltpu.matmul_pop(accs[1])
        for c in range(ci):
            if c == ci - 1:
                pl.semaphore_wait(barrier, everyone)
                for cp in hid_out:
                    cp.start()
            loads[("pi", c)].wait()
            loads[("a", c)].wait()
            tiles(pin_v, acts_v, c * gi, gi, accs[2:])
        inner_v[...] = pltpu.matmul_pop(accs[2]) + pltpu.matmul_pop(accs[3])

    pl.run_scoped(project, *[pltpu.ACC(u)((width, tokens), F32) for u in (0, 1, 0, 1)])
    for d in range(1, H):
        ph = lax.rem(h + d, H)
        cp = pltpu.make_async_remote_copy(
            inner_v.at[pl.ds(pl.multiple_of(ph * slab, slab), slab), :], inner_r.at[d - 1],
            hs_sem.at[1, d - 1], hr_sem.at[1, d - 1],
            device_id=(t, ph), device_id_type=MESH)
        cp.start()
        hid_in.append(cp)
    loads["ids"].wait()

    for cp in hid_out:
        cp.wait_recv()
    outer = outer_v[...]
    for d in range(1, H):
        outer = outer + outer_r[d - 1]
    o_hi, o_lo = split(jnp.concatenate([outer, outer], axis=0))
    for cp in hid_in:
        cp.wait_recv()
    inner = inner_v[pl.ds(pl.multiple_of(h * slab, slab), slab), :]
    for d in range(1, H):
        inner = inner + inner_r[d - 1]
    for e in range(E):
        w_v[pl.ds(e * slab, slab), :] = inner * (ids_v[...] == e).astype(F32)

    def combine(*accs):
        o = jnp.concatenate([o_hi, o_lo], axis=0)
        for unit, w in enumerate(split(w_v[...])):
            for j in range(0, tokens, TILE):
                slot = j // TILE % 2
                pltpu.matmul_push_rhs(o[:, j:j + TILE], slot, unit, transpose=True)
                pltpu.matmul_acc_lhs(accs[unit], w[:, j:j + TILE], slot)
        r = pltpu.matmul_pop(accs[0]) + pltpu.matmul_pop(accs[1])
        r_v[...] = r[:, :2 * width] + r[:, 2 * width:]

    pl.run_scoped(combine, *[pltpu.ACC(u)((E * slab, TILE), F32) for u in (0, 1)])
    left = lax.broadcasted_iota(jnp.int32, (E, 2 * width), 1) < width
    for n in range(half):
        y_v[n] = jnp.where(
            left, r_v[pl.ds(2 * n, E, stride=slab), :], r_v[pl.ds(2 * n + 1, E, stride=slab), :])

    def band(i):
        return pl.ds(i * part, part)

    send = []
    for d in range(1, A):
        pa = lax.rem(a + d, A)
        cp = pltpu.make_async_remote_copy(
            y_v.at[band(pa)], rs_r.at[d - 1], as_sem, ar_sem,
            device_id=(b * A + pa, h), device_id_type=MESH)
        cp.start()
        send.append(cp)
    loads["p"].wait()
    M = p_v.shape[0]
    fill((p_hi, p_lo), p_v, (pl.ds(0, M), slice(None)))
    loads["q"].wait()
    fill((q_hi, q_lo), q_v, (slice(None), pl.ds(0, M)))
    f2_v[...] = jnp.zeros(f2_v.shape, F32)
    im2_v[...] = jnp.zeros(im2_v.shape, F32)
    mine = y_v[band(a)]
    every = pltpu.make_async_copy(rs_r, rs_r, ar_sem)
    every.wait()
    for d in range(1, A):
        mine = mine + rs_r[d - 1]
    all_v[b, band(a)] = mine
    each = TILE // (2 * width)
    opt = each // part

    def gather(db, da):
        pb, pa = lax.rem(b + db, B), lax.rem(a + da, A)
        return pltpu.make_async_remote_copy(
            all_v.at[b, band(a)], all_v.at[b, band(a)], gs_sem, gr_sem.at[b, lax.div(a, opt)],
            device_id=(pb * A + pa, h), device_id_type=MESH)

    for db in sorted(range(B), key=lambda g: -min(g, B - g)):
        for da in range(A)[::-1]:
            if db or da:
                gather(db, da).start()
    lanes = 2 * width
    cuts = half * lanes // TILE
    Q = q_hi.shape[0]
    span = Q // T
    deep = E * span // 128

    def score(im_hi, im_lo, *outs):
        G = min(4, cuts)
        first = lax.div(a, opt)
        turn = []
        for d in range(cuts):
            far = lax.rem(lax.div(first, G) + d // G, cuts // G)
            turn.append(far * G + lax.rem(lax.rem(first, G) + d % G, G))
        rows = [pl.ds(pl.multiple_of(j * TILE, TILE), TILE) for j in turn]

        def push(n):
            for unit, p in enumerate((p_hi, p_lo)):
                pltpu.matmul_push_rhs(p[:, rows[n]], n % 2, unit, transpose=True)

        def push_q(n):
            for slot, q in enumerate((q_hi, q_lo)):
                pltpu.matmul_push_rhs(q[pl.ds(n * TILE, TILE), :], slot, n % 2, transpose=True)

        for n in range(min(2, len(rows))):
            push(n)
        for d in range(cuts):
            for db in range(B):
                n = each if d or db else each - part
                if n:
                    got = all_v.at[0, pl.ds(0, n)]
                    pltpu.make_async_copy(got, got, gr_sem.at[lax.rem(b + db, B), turn[d]]).wait()
            at = pl.ds(turn[d] * each, each)
            total = all_v[0, at]
            for i in range(1, B):
                total = total + all_v[i, at]
            full_v[at] = total
            f = jnp.concatenate([total[i] for i in range(each)], axis=1)
            f2_v[d, pl.ds(0, E), :] = f
            f2_v[d, pl.ds(E, E), :] = f - f.astype(BF).astype(F32)
            fb = f2_v[d].astype(BF)
            for acc in (im_hi, im_lo):
                pltpu.matmul_acc_lhs(acc, fb, d % 2)
            if d + 2 < cuts:
                push(d + 2)
        for n in range(min(2, Q // TILE)):
            push_q(n)
        im = pltpu.matmul_pop(im_hi) + pltpu.matmul_pop(im_lo)
        im = im[:E, :M] + im[E:2 * E, :M]
        im2_v[pl.ds(0, E), pl.ds(0, M)] = im
        im2_v[pl.ds(E, E), pl.ds(0, M)] = im - im.astype(BF).astype(F32)
        ib = im2_v[...].astype(BF)
        for n in range(Q // TILE):
            for slot in range(2):
                pltpu.matmul_acc_lhs(outs[n], ib, slot)
            if n + 2 < Q // TILE:
                push_q(n + 2)
        for n in range(Q // TILE):
            sc = pltpu.matmul_pop(outs[n])
            sc = sc[:E] + sc[E:2 * E]
            for i in range(TILE // span):
                at = slice(i * span, (i + 1) * span)
                sc_v[n * (TILE // span) + i] = jnp.concatenate(
                    [sc[j:j + deep, at] for j in range(0, E, deep)], axis=1)

    tall = im2_v.shape[0]
    pl.run_scoped(
        score,
        *[pltpu.ACC(u)((tall, TILE), F32) for u in (0, 1)],
        *[pltpu.ACC(n % 2)((tall, TILE), F32) for n in range(Q // TILE)])
    me = t * H + h

    def ssend(d):
        pt = lax.rem(t + lax.rem(d, T), T)
        ph = lax.rem(h + lax.div(d, T), H)
        return pltpu.make_async_remote_copy(
            sc_v.at[pt], s_v.at[me], ss_sem, sr_sem,
            device_id=(pt, ph), device_id_type=MESH)

    def loop(fn):
        lax.fori_loop(1, T * H, lambda d, c: (fn(d), c)[1], 0, unroll=T * H <= 32)

    loop(lambda d: ssend(d).start())
    s_v[me] = sc_v[t]
    for cp in hid_out + hid_in:
        cp.wait_send()
    for n in range(half):
        feats_out[:, pl.ds(n * lanes, lanes)] = full_v[n]
    got = s_v.at[pl.ds(0, T * H - 1)]
    pltpu.make_async_copy(got, got, sr_sem).wait()
    if T * H <= 32:
        parts = [s_v[i] for i in range(T * H)]
        while len(parts) > 1:
            parts = [parts[i] + parts[i + 1] for i in range(0, len(parts), 2)]
        tot = parts[0]
    else:
        tot = lax.fori_loop(0, T * H, lambda i, c: c + s_v[i], jnp.zeros(s_v.shape[1:], F32))
    res = jnp.concatenate([tot[:, i * span:(i + 1) * span] for i in range(E // deep)], axis=0)
    scores_out[...] = res
    pltpu.make_async_copy(got, got, ss_sem).wait()
    pltpu.make_async_copy(rs_r, rs_r, as_sem).wait()
    for n in [half] * (B - 1) + [half - part]:
        got = all_v.at[0, pl.ds(0, n)]
        pltpu.make_async_copy(got, got, gs_sem).wait()


def finish(scores, feats, scores_out, feats_out):
    scores_out[...] = scores[...]
    feats_out[...] = feats[...]


def on_device(T, H, acts, out_grads, proj_in, proj_out, example_ids, queries, precond):
    tokens = acts.shape[0]
    E = 2 * tokens * T // EX_LEN
    width = proj_in.shape[1]
    slab = width // H
    half = slab // 2
    A = min(T, half, 8)
    B = T // A
    part = half // A
    lanes = 2 * width
    cols = slab * width
    Q, M = queries.shape
    ci, co = 7, 2
    tall = -(-2 * E // 16) * 16
    deep = E * (Q // T) // 128
    cuts = half * lanes // TILE
    D = pltpu.SemaphoreType.DMA
    V = pltpu.VMEM
    hbm = pl.BlockSpec(memory_space=pltpu.HBM)
    scores, feats = pl.pallas_call(
        functools.partial(kernel, T, H, A, E, ci, co),
        out_shape=(
            jax.ShapeDtypeStruct((E, Q // T), F32),
            jax.ShapeDtypeStruct((E, cols), F32),
        ),
        in_specs=[hbm] * 7,
        out_specs=(pl.BlockSpec(memory_space=pltpu.VMEM),) * 2,
        scratch_shapes=[
            V(acts.shape, BF), V(out_grads.shape, BF),
            V(proj_in.shape[::-1], BF), V(proj_out.shape[::-1], BF),
            V((1, tokens), jnp.int32), V((Q, M), F32), V(precond.shape, F32),
            V((Q, TILE), BF), V((Q, TILE), BF),
            V((TILE, precond.shape[1]), BF), V((TILE, precond.shape[1]), BF),
            V((width, tokens), F32), V((width, tokens), F32),
            V((H - 1, slab, tokens), F32), V((H - 1, width, tokens), F32),
            V((E * slab, lanes), F32), V((E * slab, tokens), F32),
            V((half, E, lanes), F32), V((A - 1, part, E, lanes), F32),
            V((B, half, E, lanes), F32), V((half, E, lanes), F32),
            V((cuts, tall, TILE), F32), V((tall, TILE), F32),
            V((T, deep, 128), F32), V((T * H, deep, 128), F32),
            D((5 + co + 2 * ci,)), D, D((2, H - 1)), D((2, H - 1)),
            D, D, D, D((B, cuts)),
            D, D,
        ],
        compiler_params=pltpu.CompilerParams(
            collective_id=0, has_side_effects=True, vmem_limit_bytes=32000 * 1024
        ),
    )(*[pltpu.with_memory_space_constraint(x, pltpu.HBM) for x in (
        acts, out_grads, proj_in.T, proj_out.T, example_ids.reshape(1, tokens), queries, precond)])
    scores, feats = pl.pallas_call(
        finish,
        out_shape=(
            jax.ShapeDtypeStruct(scores.shape, F32),
            jax.ShapeDtypeStruct(feats.shape, F32),
        ),
        compiler_params=pltpu.CompilerParams(vmem_limit_bytes=1024 * 1024),
    )(scores, feats)
    return scores.T, feats


def solution(mesh):
    T, H = mesh.shape["tok"], mesh.shape["hid"]
    in_specs = (
        P("tok", "hid"),
        P("tok", "hid"),
        P("hid", None),
        P("hid", None),
        P("tok"),
        P(None, "tok"),
        P("tok", "hid"),
    )
    out_specs = (P("tok", None), P(None, "hid"))
    return jax.shard_map(
        functools.partial(on_device, T, H), mesh=mesh, in_specs=in_specs, out_specs=out_specs,
        check_vma=False,
    )
```

```python
import functools

import jax
import jax.numpy as jnp
from jax import lax
from jax.experimental import pallas as pl
from jax.experimental.pallas import tpu as pltpu
from jax.sharding import PartitionSpec as P

EX_LEN = 2048
TILE = 256
MESH = pl.DeviceIdType.MESH
BF, F32 = jnp.bfloat16, jnp.float32


def split(x):
    hi = x.astype(BF)
    return hi, (x - hi.astype(F32)).astype(BF)


def fill(pair, src, at):
    for ref in pair:
        if ref.shape != src.shape:
            ref[...] = jnp.zeros(ref.shape, BF)
    for ref, half in zip(pair, split(src[...])):
        ref[at] = half


def kernel(
    T, H, A, E, ci, co,
    acts, grads, pin, pout, ids, queries, precond,
    scores_out, feats_out,
    acts_v, grads_v, pin_v, pout_v, ids_v, q_v, p_v,
    q_hi, q_lo, p_hi, p_lo,
    inner_v, outer_v, inner_r, outer_r, r_v, w_v, y_v, rs_r, all_v, full_v,
    f2_v, im2_v, sc_v, s_v,
    ld_sem, in_sem, hs_sem, hr_sem, as_sem, ar_sem, gs_sem, gr_sem,
    ss_sem, sr_sem,
):
    B = T // A
    t, h = lax.axis_index("tok"), lax.axis_index("hid")
    a, b = lax.rem(t, A), lax.div(t, A)
    width, tokens = inner_v.shape
    slab = width // H
    half = slab // 2
    part = half // A

    loads = {}

    def load(name, src, dst):
        c = pltpu.make_async_copy(src, dst, ld_sem.at[len(loads)])
        c.start()
        loads[name] = c

    load("pout", pout, pout_v)
    go = grads.shape[1] // co
    for c in range(co):
        k = pl.ds(c * go, go)
        load(("g", c), grads.at[:, k], grads_v.at[:, k])
    gi = acts.shape[1] // ci
    for c in range(ci):
        k = pl.ds(c * gi, gi)
        load(("pi", c), pin.at[:, k], pin_v.at[:, k])
        load(("a", c), acts.at[:, k], acts_v.at[:, k])
    load("ids", ids, ids_v)
    load("p", precond, p_v)
    load("q", queries, q_v)

    def peer(d):
        return lax.rem(t + d // H, T), lax.rem(h + d % H, H)

    barrier = pltpu.get_barrier_semaphore()
    everyone = T * H - 1

    def greet(d, _):
        pt = lax.rem(t + lax.div(d, H), T)
        ph = lax.rem(h + lax.rem(d, H), H)
        pl.semaphore_signal(barrier, inc=1, device_id=(pt, ph), device_id_type=MESH)
        return 0

    lax.fori_loop(1, T * H, greet, 0, unroll=T * H <= 32)

    hid_out, hid_in = [], []
    for d in range(1, H):
        hid_out.append(pltpu.make_async_remote_copy(
            outer_v, outer_r.at[d - 1], hs_sem.at[0, d - 1], hr_sem.at[0, d - 1],
            device_id=(t, lax.rem(h + d, H)), device_id_type=MESH))

    def project(*accs):
        step = 0

        def tiles(x, y, start, size, pair):
            nonlocal step
            for j in range(0, size, TILE):
                k = pl.ds(start + j, TILE)
                unit, slot = step % 2, step // 2 % 2
                pltpu.matmul_push_rhs(y[:, k], slot, unit, transpose=True)
                pltpu.matmul_acc_lhs(pair[unit], x[:, k], slot)
                step += 1

        loads["pout"].wait()
        for c in range(co):
            loads[("g", c)].wait()
            tiles(pout_v, grads_v, c * go, go, accs[:2])
        outer_v[...] = pltpu.matmul_pop(accs[0]) + pltpu.matmul_pop(accs[1])
        for c in range(ci):
            if c == ci - 1:
                pl.semaphore_wait(barrier, everyone)
                for cp in hid_out:
                    cp.start()
            loads[("pi", c)].wait()
            loads[("a", c)].wait()
            tiles(pin_v, acts_v, c * gi, gi, accs[2:])
        inner_v[...] = pltpu.matmul_pop(accs[2]) + pltpu.matmul_pop(accs[3])

    pl.run_scoped(project, *[pltpu.ACC(u)((width, tokens), F32) for u in (0, 1, 0, 1)])
    for d in range(1, H):
        ph = lax.rem(h + d, H)
        cp = pltpu.make_async_remote_copy(
            inner_v.at[pl.ds(pl.multiple_of(ph * slab, slab), slab), :], inner_r.at[d - 1],
            hs_sem.at[1, d - 1], hr_sem.at[1, d - 1],
            device_id=(t, ph), device_id_type=MESH)
        cp.start()
        hid_in.append(cp)
    loads["ids"].wait()

    for cp in hid_out:
        cp.wait_recv()
    outer = outer_v[...]
    for d in range(1, H):
        outer = outer + outer_r[d - 1]
    o_hi, o_lo = split(jnp.concatenate([outer, outer], axis=0))
    for cp in hid_in:
        cp.wait_recv()
    inner = inner_v[pl.ds(pl.multiple_of(h * slab, slab), slab), :]
    for d in range(1, H):
        inner = inner + inner_r[d - 1]
    for e in range(E):
        w_v[pl.ds(e * slab, slab), :] = inner * (ids_v[...] == e).astype(F32)

    def combine(*accs):
        o = jnp.concatenate([o_hi, o_lo], axis=0)
        for unit, w in enumerate(split(w_v[...])):
            for j in range(0, tokens, TILE):
                slot = j // TILE % 2
                pltpu.matmul_push_rhs(o[:, j:j + TILE], slot, unit, transpose=True)
                pltpu.matmul_acc_lhs(accs[unit], w[:, j:j + TILE], slot)
        r = pltpu.matmul_pop(accs[0]) + pltpu.matmul_pop(accs[1])
        r_v[...] = r[:, :2 * width] + r[:, 2 * width:]

    pl.run_scoped(combine, *[pltpu.ACC(u)((E * slab, TILE), F32) for u in (0, 1)])
    left = lax.broadcasted_iota(jnp.int32, (E, 2 * width), 1) < width
    for n in range(half):
        y_v[n] = jnp.where(
            left, r_v[pl.ds(2 * n, E, stride=slab), :], r_v[pl.ds(2 * n + 1, E, stride=slab), :])

    def band(i):
        return pl.ds(i * part, part)

    send = []
    for d in range(1, A):
        pa = lax.rem(a + d, A)
        cp = pltpu.make_async_remote_copy(
            y_v.at[band(pa)], rs_r.at[d - 1], as_sem, ar_sem,
            device_id=(b * A + pa, h), device_id_type=MESH)
        cp.start()
        send.append(cp)
    loads["p"].wait()
    M = p_v.shape[0]
    fill((p_hi, p_lo), p_v, (pl.ds(0, M), slice(None)))
    loads["q"].wait()
    fill((q_hi, q_lo), q_v, (slice(None), pl.ds(0, M)))
    f2_v[...] = jnp.zeros(f2_v.shape, F32)
    im2_v[...] = jnp.zeros(im2_v.shape, F32)
    mine = y_v[band(a)]
    every = pltpu.make_async_copy(rs_r, rs_r, ar_sem)
    every.wait()
    for d in range(1, A):
        mine = mine + rs_r[d - 1]
    all_v[b, band(a)] = mine
    each = TILE // (2 * width)
    opt = each // part

    def gather(db, da):
        pb, pa = lax.rem(b + db, B), lax.rem(a + da, A)
        return pltpu.make_async_remote_copy(
            all_v.at[b, band(a)], all_v.at[b, band(a)], gs_sem, gr_sem.at[b, lax.div(a, opt)],
            device_id=(pb * A + pa, h), device_id_type=MESH)

    for db in sorted(range(B), key=lambda g: -min(g, B - g)):
        for da in range(A)[::-1]:
            if db or da:
                gather(db, da).start()
    lanes = 2 * width
    cuts = half * lanes // TILE
    Q = q_hi.shape[0]
    span = Q // T
    deep = E * span // 128
    stripes, owners = Q // TILE, TILE // span
    me = t * H + h

    def stripe(n):
        return lax.rem(lax.div(t, owners) + n + 1, stripes)

    def ssend(base, d):
        pt = base + lax.rem(lax.rem(t, owners) + lax.rem(d, owners), owners)
        ph = lax.rem(h + lax.div(d, owners), H)
        return pltpu.make_async_remote_copy(
            sc_v.at[pt], s_v.at[me], ss_sem, sr_sem, device_id=(pt, ph), device_id_type=MESH)

    def ship(n, sc):
        base = stripe(n) * owners
        sc = sc[:E] + sc[E:2 * E]
        for i in range(owners):
            at = slice(i * span, (i + 1) * span)
            sc_v[base + i] = jnp.concatenate(
                [sc[j:j + deep, at] for j in range(0, E, deep)], axis=1)
        lax.fori_loop(
            1 if n == stripes - 1 else 0, owners * H,
            lambda d, c: (ssend(base, d).start(), c)[1], 0, unroll=T * H <= 32)

    def score(im_hi, im_lo, *outs):
        G = min(4, cuts)
        first = lax.div(a, opt)
        turn = []
        for d in range(cuts):
            far = lax.rem(lax.div(first, G) + d // G, cuts // G)
            turn.append(far * G + lax.rem(lax.rem(first, G) + d % G, G))
        rows = [pl.ds(pl.multiple_of(j * TILE, TILE), TILE) for j in turn]

        def push(n):
            for unit, p in enumerate((p_hi, p_lo)):
                pltpu.matmul_push_rhs(p[:, rows[n]], n % 2, unit, transpose=True)

        def push_q(n):
            for slot, q in enumerate((q_hi, q_lo)):
                k = pl.ds(pl.multiple_of(stripe(n) * TILE, TILE), TILE)
                pltpu.matmul_push_rhs(q[k, :], slot, n % 2, transpose=True)

        for n in range(min(2, len(rows))):
            push(n)
        for d in range(cuts):
            for db in range(B):
                n = each if d or db else each - part
                if n:
                    got = all_v.at[0, pl.ds(0, n)]
                    pltpu.make_async_copy(got, got, gr_sem.at[lax.rem(b + db, B), turn[d]]).wait()
            at = pl.ds(turn[d] * each, each)
            total = all_v[0, at]
            for i in range(1, B):
                total = total + all_v[i, at]
            full_v[at] = total
            f = jnp.concatenate([total[i] for i in range(each)], axis=1)
            f2_v[d, pl.ds(0, E), :] = f
            f2_v[d, pl.ds(E, E), :] = f - f.astype(BF).astype(F32)
            fb = f2_v[d].astype(BF)
            for acc in (im_hi, im_lo):
                pltpu.matmul_acc_lhs(acc, fb, d % 2)
            if d + 2 < cuts:
                push(d + 2)
        for n in range(min(2, Q // TILE)):
            push_q(n)
        im = pltpu.matmul_pop(im_hi) + pltpu.matmul_pop(im_lo)
        im = im[:E, :M] + im[E:2 * E, :M]
        im2_v[pl.ds(0, E), pl.ds(0, M)] = im
        im2_v[pl.ds(E, E), pl.ds(0, M)] = im - im.astype(BF).astype(F32)
        ib = im2_v[...].astype(BF)
        for n in range(stripes):
            for slot in range(2):
                pltpu.matmul_acc_lhs(outs[n], ib, slot)
            if n + 2 < stripes:
                push_q(n + 2)
            if n % 2 or n == stripes - 1:
                for m in range(n - n % 2, n + 1):
                    ship(m, pltpu.matmul_pop(outs[m]))

    tall = im2_v.shape[0]
    pl.run_scoped(
        score,
        *[pltpu.ACC(u)((tall, TILE), F32) for u in (0, 1)],
        *[pltpu.ACC(n % 2)((tall, TILE), F32) for n in range(Q // TILE)])
    s_v[me] = sc_v[t]
    for cp in hid_out + hid_in:
        cp.wait_send()
    for n in range(half):
        feats_out[:, pl.ds(n * lanes, lanes)] = full_v[n]
    got = s_v.at[pl.ds(0, T * H - 1)]
    pltpu.make_async_copy(got, got, sr_sem).wait()
    if T * H <= 32:
        parts = [s_v[i] for i in range(T * H)]
        while len(parts) > 1:
            parts = [parts[i] + parts[i + 1] for i in range(0, len(parts), 2)]
        tot = parts[0]
    else:
        tot = lax.fori_loop(0, T * H, lambda i, c: c + s_v[i], jnp.zeros(s_v.shape[1:], F32))
    res = jnp.concatenate([tot[:, i * span:(i + 1) * span] for i in range(E // deep)], axis=0)
    scores_out[...] = res
    pltpu.make_async_copy(got, got, ss_sem).wait()
    pltpu.make_async_copy(rs_r, rs_r, as_sem).wait()
    for n in [half] * (B - 1) + [half - part]:
        got = all_v.at[0, pl.ds(0, n)]
        pltpu.make_async_copy(got, got, gs_sem).wait()


def finish(scores, feats, scores_out, feats_out):
    scores_out[...] = scores[...]
    feats_out[...] = feats[...]


def on_device(T, H, acts, out_grads, proj_in, proj_out, example_ids, queries, precond):
    tokens = acts.shape[0]
    E = 2 * tokens * T // EX_LEN
    width = proj_in.shape[1]
    slab = width // H
    half = slab // 2
    A = min(T, half, 8)
    B = T // A
    part = half // A
    lanes = 2 * width
    cols = slab * width
    Q, M = queries.shape
    ci, co = 7, 2
    tall = -(-2 * E // 16) * 16
    deep = E * (Q // T) // 128
    cuts = half * lanes // TILE
    D = pltpu.SemaphoreType.DMA
    V = pltpu.VMEM
    hbm = pl.BlockSpec(memory_space=pltpu.HBM)
    scores, feats = pl.pallas_call(
        functools.partial(kernel, T, H, A, E, ci, co),
        out_shape=(
            jax.ShapeDtypeStruct((E, Q // T), F32),
            jax.ShapeDtypeStruct((E, cols), F32),
        ),
        in_specs=[hbm] * 7,
        out_specs=(pl.BlockSpec(memory_space=pltpu.VMEM),) * 2,
        scratch_shapes=[
            V(acts.shape, BF), V(out_grads.shape, BF),
            V(proj_in.shape[::-1], BF), V(proj_out.shape[::-1], BF),
            V((1, tokens), jnp.int32), V((Q, M), F32), V(precond.shape, F32),
            V((Q, TILE), BF), V((Q, TILE), BF),
            V((TILE, precond.shape[1]), BF), V((TILE, precond.shape[1]), BF),
            V((width, tokens), F32), V((width, tokens), F32),
            V((H - 1, slab, tokens), F32), V((H - 1, width, tokens), F32),
            V((E * slab, lanes), F32), V((E * slab, tokens), F32),
            V((half, E, lanes), F32), V((A - 1, part, E, lanes), F32),
            V((B, half, E, lanes), F32), V((half, E, lanes), F32),
            V((cuts, tall, TILE), F32), V((tall, TILE), F32),
            V((T, deep, 128), F32), V((T * H, deep, 128), F32),
            D((5 + co + 2 * ci,)), D, D((2, H - 1)), D((2, H - 1)),
            D, D, D, D((B, cuts)),
            D, D,
        ],
        compiler_params=pltpu.CompilerParams(
            collective_id=0, has_side_effects=True, vmem_limit_bytes=32000 * 1024
        ),
    )(*[pltpu.with_memory_space_constraint(x, pltpu.HBM) for x in (
        acts, out_grads, proj_in.T, proj_out.T, example_ids.reshape(1, tokens), queries, precond)])
    scores, feats = pl.pallas_call(
        finish,
        out_shape=(
            jax.ShapeDtypeStruct(scores.shape, F32),
            jax.ShapeDtypeStruct(feats.shape, F32),
        ),
        compiler_params=pltpu.CompilerParams(vmem_limit_bytes=1024 * 1024),
    )(scores, feats)
    return scores.T, feats


def solution(mesh):
    T, H = mesh.shape["tok"], mesh.shape["hid"]
    in_specs = (
        P("tok", "hid"),
        P("tok", "hid"),
        P("hid", None),
        P("hid", None),
        P("tok"),
        P(None, "tok"),
        P("tok", "hid"),
    )
    out_specs = (P("tok", None), P(None, "hid"))
    return jax.shard_map(
        functools.partial(on_device, T, H), mesh=mesh, in_specs=in_specs, out_specs=out_specs,
        check_vma=False,
    )
```
